32 devices in a mesh: row: 4 (over y, x), col: 8 (over z, core).
Axes of the slice: x: 2, y: 2, z: 4, core: 2. Of those that a mesh axis runs over, the one named last changes fastest.
Arguments:
- node_features: bfloat16 [2048, 128, 512], P(('row', 'col')), may hold values from -6 to 6
- node_counts: int32 [2048], P(('row', 'col')), may hold values from 16 to 128, as said below
- edge_list: int32 [2048, 2, 256], P(('row', 'col')), may hold values from 0 to 128, as said below
- readout_ids: int32 [2048], P(('row', 'col')), may hold values from 0 to 255
- live_graphs: int32 [32], P(('row', 'col')), may hold values from 1 to 64, as said below
- self_weight: float32 [1], replicated, may hold values from 0.5 to 1.5
- w_first: bfloat16 [512, 512], replicated, may hold values from -0.25 to 0.25
- b_first: float32 [512], replicated, may hold values from -3 to 3
- w_second: bfloat16 [512, 512], replicated, may hold values from -0.25 to 0.25
- b_second: float32 [512], replicated, may hold values from -3 to 3
- w_third: bfloat16 [512, 512], replicated, may hold values from -0.25 to 0.25
- b_third: float32 [512], replicated, may hold values from -3 to 3
Outputs:
- node_out: bfloat16 [1024, 128, 512], P(('row', 'col'))
- readout: float32 [256, 512], P(('row', 'col'))
The draws below stay inside these ranges and needn't reach their ends.
Inputs may be any that keep to these rules, and one draw needn't show every extreme that they name: `live_graphs`: the entries sum to 1024, and at least one equals 64. `node_counts`: node slots 0 to count - 1 of a graph are live; the rest of its block is padding. `edge_list`: each edge slot holds two node indices below its graph's node count, or 128 in both rows for an unused slot.
All inputs are finite; a program needn't handle non-finite values.
Results may differ from the reference program's by a relative error of at most 0.0058.
Values may be sent and summed in bfloat16 or wider, within the bound.
A program may use at most 128 MiB of HBM per device.

```python
import jax
import jax.numpy as jnp
from jax import lax

H = 512
BLOCK = 128
G_DEV = 32
MIN_NODES = 16
CAP_IN = 64
GRAPHS = 1024
GRAPHS_IN = 2048
READOUTS = 256
DEVICES = 32


def graph_shapes(key):
    folded = jax.random.fold_in(key, 11)
    counts = jax.random.randint(jax.random.fold_in(folded, 1), (GRAPHS_IN,), MIN_NODES, BLOCK + 1, dtype=jnp.int32)
    pair_total = jax.random.randint(jax.random.fold_in(folded, 2), (GRAPHS_IN,), counts // 2, counts + 1, dtype=jnp.int32)
    ends_first = jax.random.randint(jax.random.fold_in(folded, 3), (GRAPHS_IN, BLOCK), 0, counts[:, None], dtype=jnp.int32)
    ends_second = jax.random.randint(jax.random.fold_in(folded, 4), (GRAPHS_IN, BLOCK), 0, counts[:, None], dtype=jnp.int32)
    pair_index = jnp.arange(BLOCK, dtype=jnp.int32)[None, :]
    pair_used = jnp.concatenate([pair_index < pair_total[:, None], pair_index < pair_total[:, None]], axis=1)
    sources = jnp.where(pair_used, jnp.concatenate([ends_first, ends_second], axis=1), BLOCK)
    targets = jnp.where(pair_used, jnp.concatenate([ends_second, ends_first], axis=1), BLOCK)
    return (counts, jnp.stack([sources, targets], axis=1).astype(jnp.int32))


def draw_node_counts(key, part):
    return graph_shapes(key)[0]


def draw_edge_list(key, part):
    return graph_shapes(key)[1]


def draw_live_graphs(key, part):
    halves = DEVICES // 2
    shuffled = jax.random.permutation(jax.random.fold_in(key, 23), DEVICES)
    moves = jax.random.randint(jax.random.fold_in(key, 29), (halves,), 0, G_DEV, dtype=jnp.int32)
    moves = moves.at[0].set(G_DEV - 1)
    higher = G_DEV + moves
    lower = G_DEV - moves
    higher = higher.at[0].add(1)
    higher = higher.at[1].add(-1)
    counts = jnp.zeros((DEVICES,), jnp.int32)
    counts = counts.at[shuffled[0::2]].set(higher)
    counts = counts.at[shuffled[1::2]].set(lower)
    return counts.astype(jnp.int32)


def set_ends(values, own_key, smallest, largest):
    extent = values.shape
    place = [jax.random.randint(jax.random.fold_in(own_key, axis), (), 0, extent[axis]) for axis in range(len(extent))]
    values = values.at[tuple(place)].set(smallest)
    longest = extent.index(max(extent))
    place[longest] = (place[longest] + 1) % extent[longest]
    return values.at[tuple(place)].set(largest)


def levels(key, shape, pieces, least, high):
    gain, own = 1.0, jax.random.fold_in(key, 6)
    for position, blocks in pieces:
        steps = jnp.exp(jax.random.uniform(jax.random.fold_in(own, position), (blocks,), jnp.float32, least / len(pieces), high / len(pieces)))
        gain = gain * jnp.repeat(steps, shape[position] // blocks).reshape([-1 if axis == position else 1 for axis in range(len(shape))])
    return gain


def normal_values(key, dims, spread, reach, pieces=(), kind=jnp.bfloat16):
    values = jax.random.normal(key, dims, jnp.float32) * spread
    if len(pieces) > 0:
        values = levels(key, dims, pieces, -0.22, 0.18) * values
    return jnp.clip(values, min=-reach, max=reach).astype(kind)


def setup_inputs(seed: int = 0) -> dict:
    splits = jax.random.split(jax.random.key(seed), 13)
    node_features = normal_values(splits[0], (GRAPHS_IN, BLOCK, H), 1.0, 6.0, ((0, 32),))
    node_counts = draw_node_counts(jax.random.fold_in(splits[12], 71), 0)
    edge_list = draw_edge_list(jax.random.fold_in(splits[12], 71), 0)
    readout_ids = set_ends(jax.random.randint(splits[3], (GRAPHS_IN,), 0, READOUTS), jax.random.fold_in(splits[3], 1), 0, READOUTS - 1).astype(jnp.int32)
    live_graphs = draw_live_graphs(jax.random.fold_in(splits[12], 71), 0)
    self_weight = jnp.clip(jax.random.uniform(splits[5], (1,), jnp.float32, 0.5, 1.5), 0.5, 1.5)
    w_first = normal_values(splits[6], (H, H), H ** -0.5, 0.25)
    b_first = normal_values(splits[7], (H,), 0.5, 3.0, (), jnp.float32)
    w_second = normal_values(splits[8], (H, H), H ** -0.5, 0.25)
    b_second = normal_values(splits[9], (H,), 0.5, 3.0, (), jnp.float32)
    w_third = normal_values(splits[10], (H, H), H ** -0.5, 0.25)
    b_third = normal_values(splits[11], (H,), 0.5, 3.0, (), jnp.float32)
    return {"node_features": node_features, "node_counts": node_counts, "edge_list": edge_list, "readout_ids": readout_ids, "live_graphs": live_graphs, "self_weight": self_weight, "w_first": w_first, "b_first": b_first, "w_second": w_second, "b_second": b_second, "w_third": w_third, "b_third": b_third}


def blend_nodes(features, edge_slots, self_weight):
    node_index = jnp.arange(BLOCK, dtype=jnp.int32)
    sources = (edge_slots[:, 0, :, None] == node_index[None, None, :]).astype(jnp.float32)
    targets = (edge_slots[:, 1, :, None] == node_index[None, None, :]).astype(jnp.float32)
    adjacency = jnp.einsum("gek,gel->gkl", targets, sources)
    neighbour = jnp.einsum("gkl,glh->gkh", adjacency, features.astype(jnp.float32))
    return (self_weight[0] * features.astype(jnp.float32) + neighbour).astype(jnp.bfloat16)


def perceptron(blended, weights):
    w_first, b_first, w_second, b_second, w_third, b_third = weights
    flat_rows = blended.reshape(-1, blended.shape[-1])
    hidden_one = jax.nn.relu(jnp.dot(flat_rows, w_first, preferred_element_type=jnp.float32) + b_first).astype(jnp.bfloat16)
    hidden_two = jax.nn.relu(jnp.dot(hidden_one, w_second, preferred_element_type=jnp.float32) + b_second).astype(jnp.bfloat16)
    result = jnp.dot(hidden_two, w_third, preferred_element_type=jnp.float32) + b_third
    return result.reshape(blended.shape)


def source_rows(live_graphs):
    inclusive = jnp.cumsum(live_graphs).astype(jnp.int32)
    offsets = (inclusive - live_graphs).astype(jnp.int32)
    order_index = jnp.arange(GRAPHS, dtype=jnp.int32)
    number = (order_index % G_DEV) * DEVICES + order_index // G_DEV
    source = jnp.sum((inclusive[None, :] <= number[:, None]).astype(jnp.int32), axis=1).astype(jnp.int32)
    return (source * CAP_IN + number - offsets[source]).astype(jnp.int32)


def reference(node_features, node_counts, edge_list, readout_ids, live_graphs, self_weight, w_first, b_first, w_second, b_second, w_third, b_third):
    weights = (w_first, b_first, w_second, b_second, w_third, b_third)
    chosen = source_rows(live_graphs).reshape(DEVICES, G_DEV)

    def one_group(indices):
        features = node_features[indices]
        counts_here = node_counts[indices]
        blended = blend_nodes(features, edge_list[indices], self_weight)
        live_nodes = jnp.arange(BLOCK, dtype=jnp.int32)[None, :] < counts_here[:, None]
        outputs = jnp.where(live_nodes[:, :, None], perceptron(blended, weights), 0.0).astype(jnp.bfloat16)
        pooled = jnp.sum(outputs.astype(jnp.float32), axis=1) / counts_here[:, None].astype(jnp.float32)
        return outputs, pooled

    node_out, pooled = lax.map(one_group, chosen)
    node_out = node_out.reshape(GRAPHS, BLOCK, H)
    pooled = pooled.reshape(GRAPHS, H)
    graph_ids = readout_ids[chosen.reshape(-1)]
    id_keys = jnp.arange(READOUTS, dtype=jnp.int32)
    members = (id_keys[:, None] == graph_ids[None, :]).astype(jnp.float32)
    readout = jnp.dot(members, pooled, precision=lax.Precision.HIGHEST, preferred_element_type=jnp.float32)
    return node_out, readout
```

```python
import functools

import jax
import jax.numpy as jnp
from jax import lax
from jax.experimental import pallas as pl
from jax.experimental.pallas import tpu as pltpu
from jax.sharding import PartitionSpec as P

MESH = pl.DeviceIdType.MESH
VMEM = pl.BlockSpec(memory_space=pltpu.VMEM)
SMEM = pl.BlockSpec(memory_space=pltpu.SMEM)


def partners(step, sizes):
    rows, cols = sizes
    row, col = lax.axis_index("row"), lax.axis_index("col")
    by_row, by_col = step // cols, (step % cols) * 3 % cols
    to_row, to_col = (row + by_row) % rows, (col + by_col) % cols
    from_row, from_col = (row + rows - by_row) % rows, (col + cols - by_col) % cols
    return (to_row, to_col), to_row * cols + to_col, from_row * cols + from_col


def greet(sizes):
    barrier = pltpu.get_barrier_semaphore()
    devices = sizes[0] * sizes[1]

    def signal(step, carry):
        where, _, _ = partners(step, sizes)
        pl.semaphore_signal(barrier, inc=1, device_id=where, device_id_type=MESH)
        return carry

    lax.fori_loop(1, devices, signal, 0)
    return barrier


def gather_kernel(sizes, own_ref, all_ref, send_sem, recv_sem):
    devices = sizes[0] * sizes[1]
    me = lax.axis_index("row") * sizes[1] + lax.axis_index("col")
    barrier = greet(sizes)
    all_ref[me] = own_ref[0]
    pl.semaphore_wait(barrier, devices - 1)

    def copy(step, slot):
        where, _, _ = partners(step, sizes)
        return pltpu.make_async_remote_copy(
            src_ref=own_ref.at[0],
            dst_ref=all_ref.at[slot],
            send_sem=send_sem.at[step],
            recv_sem=recv_sem.at[step],
            device_id=where,
            device_id_type=MESH,
        )

    def send(step, carry):
        copy(step, me).start()
        return carry

    def finish(step, carry):
        _, _, source = partners(step, sizes)
        copy(step, me).wait_send()
        copy(step, source).wait_recv()
        return carry

    lax.fori_loop(1, devices, send, 0)
    lax.fori_loop(1, devices, finish, 0)


def gather_counts(live_graphs, sizes):
    devices = sizes[0] * sizes[1]
    own = jnp.broadcast_to(live_graphs.reshape(1, 1, 1), (1, 1, 128))
    every = pl.pallas_call(
        functools.partial(gather_kernel, sizes),
        out_shape=jax.ShapeDtypeStruct((devices, 1, 128), jnp.int32),
        in_specs=[VMEM],
        out_specs=VMEM,
        scratch_shapes=[
            pltpu.SemaphoreType.DMA((devices,)),
            pltpu.SemaphoreType.DMA((devices,)),
        ],
        compiler_params=pltpu.CompilerParams(collective_id=0, has_side_effects=True),
        name="gather_counts",
    )(own)
    return every[:, 0, 0]


def layer_kernel(
    sizes,
    bucket,
    picked_ref,
    counts_ref,
    arrival_ref,
    weight_ref,
    features_ref,
    edges_ref,
    ids_ref,
    w_first_ref,
    b_first_ref,
    w_second_ref,
    b_second_ref,
    w_third_ref,
    b_third_ref,
    out_ref,
    readout_ref,
    sent,
    arrived,
    pooled,
    terms,
    terms_in,
    send_sem,
    recv_sem,
    terms_send_sem,
    terms_recv_sem,
):
    devices = sizes[0] * sizes[1]
    read_rows = readout_ref.shape[0]
    block, hidden = features_ref.shape[1:]
    me = lax.axis_index("row") * sizes[1] + lax.axis_index("col")
    barrier = greet(sizes)

    def graph_copy(step, target, slot):
        where, _, _ = partners(step, sizes)
        return pltpu.make_async_remote_copy(
            src_ref=sent.at[target],
            dst_ref=arrived.at[slot],
            send_sem=send_sem.at[step],
            recv_sem=recv_sem.at[step],
            device_id=where,
            device_id_type=MESH,
        )

    def terms_copy(step, target, slot):
        where, _, _ = partners(step, sizes)
        return pltpu.make_async_remote_copy(
            src_ref=terms.at[target],
            dst_ref=terms_in.at[slot],
            send_sem=terms_send_sem.at[step],
            recv_sem=terms_recv_sem.at[step],
            device_id=where,
            device_id_type=MESH,
        )

    node_rows = lax.broadcasted_iota(jnp.int32, (block, edges_ref.shape[2]), 0)
    node_index = lax.broadcasted_iota(jnp.int32, (block, hidden), 0)

    def compute(target, store):
        blends = []
        for j in range(bucket):
            graph = picked_ref[target * bucket + j]
            features = features_ref[graph]
            edges = edges_ref[graph]
            sources = (node_rows == edges[0:1, :]).astype(jnp.float32).astype(jnp.bfloat16)
            targets = (node_rows == edges[1:2, :]).astype(jnp.float32).astype(jnp.bfloat16)
            adjacency = lax.dot_general(
                targets,
                sources,
                (((1,), (1,)), ((), ())),
                preferred_element_type=jnp.float32,
            ).astype(jnp.bfloat16)
            neighbour = jnp.dot(adjacency, features, preferred_element_type=jnp.float32)
            blends.append(
                (weight_ref[0] * features.astype(jnp.float32) + neighbour).astype(jnp.bfloat16)
            )
        blended = jnp.concatenate(blends, axis=0) if bucket > 1 else blends[0]
        hidden_one = jnp.maximum(
            jnp.dot(blended, w_first_ref[...], preferred_element_type=jnp.float32)
            + b_first_ref[...],
            0.0,
        ).astype(jnp.bfloat16)
        hidden_two = jnp.maximum(
            jnp.dot(hidden_one, w_second_ref[...], preferred_element_type=jnp.float32)
            + b_second_ref[...],
            0.0,
        ).astype(jnp.bfloat16)
        result = (
            jnp.dot(hidden_two, w_third_ref[...], preferred_element_type=jnp.float32)
            + b_third_ref[...]
        )
        for j in range(bucket):
            count = counts_ref[target * bucket + j]
            rows = jnp.where(node_index < count, result[j * block : (j + 1) * block], 0.0)
            rows = rows.astype(jnp.bfloat16)
            store(j, rows)
            total = jnp.sum(rows.astype(jnp.float32), axis=0, keepdims=True)
            pooled[target * bucket + j] = total / jnp.full((1, hidden), count).astype(jnp.float32)

    pl.semaphore_wait(barrier, devices - 1)

    def compute_and_send(step, carry):
        _, target, _ = partners(step, sizes)

        def store(j, rows):
            sent[target, j] = rows

        compute(target, store)
        graph_copy(step, target, me).start()
        return carry

    lax.fori_loop(1, devices, compute_and_send, 0)

    def store_own(j, rows):
        arrived[me, j] = rows

    compute(me, store_own)

    slots = devices * bucket
    keys = lax.broadcasted_iota(jnp.int32, (devices * read_rows, slots), 0)
    members = (keys == ids_ref[...]).astype(jnp.float32)
    all_terms = jnp.dot(
        members,
        pooled[...].reshape(slots, hidden),
        precision=lax.Precision.HIGHEST,
        preferred_element_type=jnp.float32,
    )
    terms[...] = all_terms.reshape(devices, read_rows, hidden)

    def send_terms(step, carry):
        _, target, _ = partners(step, sizes)
        terms_copy(step, target, me).start()
        return carry

    lax.fori_loop(1, devices, send_terms, 0)
    terms_in[me] = terms[me]

    def finish(step, carry):
        _, target, source = partners(step, sizes)
        graph_copy(step, target, me).wait_send()
        graph_copy(step, target, source).wait_recv()
        terms_copy(step, target, me).wait_send()
        terms_copy(step, target, source).wait_recv()
        return carry

    lax.fori_loop(1, devices, finish, 0)
    readout_ref[...] = jnp.sum(terms_in[...], axis=0)

    def place(slot, carry):
        which = arrival_ref[slot]
        out_ref[slot] = arrived[which // bucket, which % bucket]
        return carry

    lax.fori_loop(0, out_ref.shape[0], place, 0)


def body(
    sizes,
    node_features,
    node_counts,
    edge_list,
    readout_ids,
    live_graphs,
    self_weight,
    w_first,
    b_first,
    w_second,
    b_second,
    w_third,
    b_third,
):
    devices = sizes[0] * sizes[1]
    capacity, block, hidden = node_features.shape
    graphs_out = capacity // 2
    read_rows = 8
    bucket = (capacity + devices - 1) // devices
    own_count = live_graphs[0]
    me = lax.axis_index(("row", "col"))
    every_count = gather_counts(live_graphs, sizes)
    inclusive = jnp.cumsum(every_count)
    offsets = inclusive - every_count
    offset = offsets[me]
    slots = lax.broadcasted_iota(jnp.int32, (devices * bucket,), 0)
    within = (slots // bucket - offset) % devices + slots % bucket * devices
    picked = jnp.minimum(within, capacity - 1)
    counts = node_counts[picked]
    graph_ids = jnp.where(within < own_count, readout_ids[picked], -1)
    number = lax.broadcasted_iota(jnp.int32, (graphs_out,), 0) * devices + me
    passed = (inclusive[None, :] <= number[:, None]).astype(jnp.int32)
    source = jnp.sum(passed, axis=1)
    start = jnp.sum(passed * every_count[None, :], axis=1)
    arrival = source * bucket + (number - start) // devices
    return pl.pallas_call(
        functools.partial(layer_kernel, sizes, bucket),
        out_shape=(
            jax.ShapeDtypeStruct((graphs_out, block, hidden), jnp.bfloat16),
            jax.ShapeDtypeStruct((read_rows, hidden), jnp.float32),
        ),
        in_specs=[SMEM] * 4 + [VMEM] * 9,
        out_specs=(VMEM, VMEM),
        scratch_shapes=[
            pltpu.VMEM((devices, bucket, block, hidden), jnp.bfloat16),
            pltpu.VMEM((devices, bucket, block, hidden), jnp.bfloat16),
            pltpu.VMEM((devices * bucket, 1, hidden), jnp.float32),
            pltpu.VMEM((devices, read_rows, hidden), jnp.float32),
            pltpu.VMEM((devices, read_rows, hidden), jnp.float32),
            pltpu.SemaphoreType.DMA((devices,)),
            pltpu.SemaphoreType.DMA((devices,)),
            pltpu.SemaphoreType.DMA((devices,)),
            pltpu.SemaphoreType.DMA((devices,)),
        ],
        compiler_params=pltpu.CompilerParams(
            collective_id=1, has_side_effects=True, vmem_limit_bytes=60 * 1024 * 1024
        ),
        name="gin_layer",
    )(
        picked,
        counts,
        arrival,
        self_weight,
        node_features,
        edge_list,
        graph_ids.reshape(1, -1),
        w_first,
        b_first.reshape(1, -1),
        w_second,
        b_second.reshape(1, -1),
        w_third,
        b_third.reshape(1, -1),
    )


def solution(mesh):
    sizes = (mesh.shape["row"], mesh.shape["col"])
    both = ("row", "col")
    in_specs = (
        P(both, None, None),
        P(both),
        P(both, None, None),
        P(both),
        P(both),
        P(),
        P(),
        P(),
        P(),
        P(),
        P(),
        P(),
    )
    out_specs = (P(both, None, None), P(both, None))
    return jax.shard_map(
        functools.partial(body, sizes),
        mesh=mesh,
        in_specs=in_specs,
        out_specs=out_specs,
        check_vma=False,
    )
```

```python
import functools

import jax
import jax.numpy as jnp
from jax import lax
from jax.experimental import pallas as pl
from jax.experimental.pallas import tpu as pltpu
from jax.sharding import PartitionSpec as P

MESH = pl.DeviceIdType.MESH
VMEM = pl.BlockSpec(memory_space=pltpu.VMEM)
SMEM = pl.BlockSpec(memory_space=pltpu.SMEM)
PLANES = 4
UNIT = 16
CLASSES = (2, 3, 1, 0)


def partners(step, sizes):
    rows, cols = sizes
    row, col = lax.axis_index("row"), lax.axis_index("col")
    by_row, by_col = step // cols, (step % cols) * 3 % cols
    to_row, to_col = (row + by_row) % rows, (col + by_col) % cols
    from_row, from_col = (row + rows - by_row) % rows, (col + cols - by_col) % cols
    return (to_row, to_col), to_row * cols + to_col, from_row * cols + from_col


def greet(sizes):
    barrier = pltpu.get_barrier_semaphore()
    devices = sizes[0] * sizes[1]

    def signal(step, carry):
        where, _, _ = partners(step, sizes)
        pl.semaphore_signal(barrier, inc=1, device_id=where, device_id_type=MESH)
        return carry

    lax.fori_loop(1, devices, signal, 0)
    return barrier


def gather_kernel(sizes, own_ref, all_ref, send_sem, recv_sem):
    devices = sizes[0] * sizes[1]
    me = lax.axis_index("row") * sizes[1] + lax.axis_index("col")
    barrier = greet(sizes)
    all_ref[me] = own_ref[0]
    pl.semaphore_wait(barrier, devices - 1)

    def copy(step, slot):
        where, _, _ = partners(step, sizes)
        return pltpu.make_async_remote_copy(
            src_ref=own_ref.at[0],
            dst_ref=all_ref.at[slot],
            send_sem=send_sem.at[step],
            recv_sem=recv_sem.at[step],
            device_id=where,
            device_id_type=MESH,
        )

    def send(step, carry):
        copy(step, me).start()
        return carry

    def finish(step, carry):
        _, _, source = partners(step, sizes)
        copy(step, me).wait_send()
        copy(step, source).wait_recv()
        return carry

    lax.fori_loop(1, devices, send, 0)
    lax.fori_loop(1, devices, finish, 0)


def gather_counts(node_counts, live_graphs, sizes):
    devices = sizes[0] * sizes[1]
    own = jnp.concatenate([node_counts, live_graphs])
    own = jnp.pad(own, (0, -own.shape[0] % 128)).reshape(1, 1, -1)
    every = pl.pallas_call(
        functools.partial(gather_kernel, sizes),
        out_shape=jax.ShapeDtypeStruct((devices, 1, own.shape[2]), jnp.int32),
        in_specs=[VMEM],
        out_specs=VMEM,
        scratch_shapes=[
            pltpu.SemaphoreType.DMA((devices,)),
            pltpu.SemaphoreType.DMA((devices,)),
        ],
        compiler_params=pltpu.CompilerParams(collective_id=0, has_side_effects=True),
        name="gather_counts",
    )(own)
    return every[:, 0, :]


def layer_kernel(
    sizes,
    bucket,
    picked_ref,
    counts_ref,
    arrival_ref,
    weight_ref,
    features_ref,
    edges_ref,
    ids_ref,
    w_first_ref,
    b_first_ref,
    w_second_ref,
    b_second_ref,
    w_third_ref,
    b_third_ref,
    out_ref,
    readout_ref,
    sent,
    arrived,
    pooled,
    terms,
    terms_in,
    send_sem,
    recv_sem,
    terms_send_sem,
    terms_recv_sem,
):
    devices = sizes[0] * sizes[1]
    read_rows = readout_ref.shape[0]
    block, hidden = features_ref.shape[1:]
    me = lax.axis_index("row") * sizes[1] + lax.axis_index("col")
    barrier = greet(sizes)

    def graph_copy(step, target, slot):
        where, _, _ = partners(step, sizes)
        return pltpu.make_async_remote_copy(
            src_ref=sent.at[target],
            dst_ref=arrived.at[slot],
            send_sem=send_sem.at[step],
            recv_sem=recv_sem.at[step],
            device_id=where,
            device_id_type=MESH,
        )

    def terms_copy(step, target, slot):
        where, _, _ = partners(step, sizes)
        return pltpu.make_async_remote_copy(
            src_ref=terms.at[target],
            dst_ref=terms_in.at[slot],
            send_sem=terms_send_sem.at[step],
            recv_sem=terms_recv_sem.at[step],
            device_id=where,
            device_id_type=MESH,
        )

    node_rows = lax.broadcasted_iota(jnp.int32, (block, edges_ref.shape[2]), 0)
    node_index = lax.broadcasted_iota(jnp.int32, (block, hidden), 0)

    def compute(target, store):
        blends = []
        for j in range(bucket):
            graph = picked_ref[target * bucket + j]
            features = features_ref[graph]
            edges = edges_ref[graph]
            sources = (node_rows == edges[0:1, :]).astype(jnp.float32).astype(jnp.bfloat16)
            targets = (node_rows == edges[1:2, :]).astype(jnp.float32).astype(jnp.bfloat16)
            adjacency = lax.dot_general(
                targets,
                sources,
                (((1,), (1,)), ((), ())),
                preferred_element_type=jnp.float32,
            ).astype(jnp.bfloat16)
            neighbour = jnp.dot(adjacency, features, preferred_element_type=jnp.float32)
            blends.append(
                (weight_ref[0] * features.astype(jnp.float32) + neighbour).astype(jnp.bfloat16)
            )
        blended = jnp.concatenate(blends, axis=0) if bucket > 1 else blends[0]
        hidden_one = jnp.maximum(
            jnp.dot(blended, w_first_ref[...], preferred_element_type=jnp.float32)
            + b_first_ref[...],
            0.0,
        ).astype(jnp.bfloat16)
        hidden_two = jnp.maximum(
            jnp.dot(hidden_one, w_second_ref[...], preferred_element_type=jnp.float32)
            + b_second_ref[...],
            0.0,
        ).astype(jnp.bfloat16)
        result = (
            jnp.dot(hidden_two, w_third_ref[...], preferred_element_type=jnp.float32)
            + b_third_ref[...]
        )
        for j in range(bucket):
            count = counts_ref[picked_ref[target * bucket + j]]
            rows = jnp.where(node_index < count, result[j * block : (j + 1) * block], 0.0)
            rows = rows.astype(jnp.bfloat16)
            store(j, rows)
            total = jnp.sum(rows.astype(jnp.float32), axis=0, keepdims=True)
            pooled[target * bucket + j] = total / jnp.full((1, hidden), count).astype(jnp.float32)

    pl.semaphore_wait(barrier, devices - 1)

    def compute_and_send(step, carry):
        _, target, _ = partners(step, sizes)

        def store(j, rows):
            sent[target, j] = rows

        compute(target, store)
        graph_copy(step, target, me).start()
        return carry

    lax.fori_loop(1, devices, compute_and_send, 0)

    def store_own(j, rows):
        arrived[me, j] = rows

    compute(me, store_own)

    slots = devices * bucket
    keys = lax.broadcasted_iota(jnp.int32, (devices * read_rows, slots), 0)
    members = (keys == ids_ref[...]).astype(jnp.float32)
    all_terms = jnp.dot(
        members,
        pooled[...].reshape(slots, hidden),
        precision=lax.Precision.HIGHEST,
        preferred_element_type=jnp.float32,
    )
    terms[...] = all_terms.reshape(devices, read_rows, hidden)

    def send_terms(step, carry):
        _, target, _ = partners(step, sizes)
        terms_copy(step, target, me).start()
        return carry

    lax.fori_loop(1, devices, send_terms, 0)
    terms_in[me] = terms[me]

    def finish(step, carry):
        _, target, source = partners(step, sizes)
        graph_copy(step, target, me).wait_send()
        graph_copy(step, target, source).wait_recv()
        terms_copy(step, target, me).wait_send()
        terms_copy(step, target, source).wait_recv()
        return carry

    lax.fori_loop(1, devices, finish, 0)
    readout_ref[...] = jnp.sum(terms_in[...], axis=0)

    def place(slot, carry):
        which = arrival_ref[slot]
        out_ref[slot] = arrived[which // bucket, which % bucket]
        return carry

    lax.fori_loop(0, out_ref.shape[0], place, 0)


def relay_kernel(
    sizes,
    bucket,
    units,
    table_ref,
    counts_ref,
    weight_ref,
    features_ref,
    edges_ref,
    ids_ref,
    w_first_ref,
    b_first_ref,
    w_second_ref,
    b_second_ref,
    w_third_ref,
    b_third_ref,
    out_ref,
    readout_ref,
    sent,
    arrived_a,
    arrived_b,
    arrived_c,
    arrived_d,
    packed,
    unpacked,
    pooled,
    terms,
    terms_in,
    send_sem,
    recv_sem,
    relay_send_sem,
    relay_recv_sem,
    terms_send_sem,
    terms_recv_sem,
):
    rows_n, cols_n = sizes
    devices = rows_n * cols_n
    width = cols_n // PLANES
    in_plane = rows_n * width
    read_rows = readout_ref.shape[0]
    block, hidden = features_ref.shape[1:]
    parts = block // UNIT
    slots = devices * bucket
    pack_at = slots
    base_at = pack_at + PLANES * units
    size_at = base_at + out_ref.shape[0]
    arrived = (arrived_a, arrived_b, arrived_c, arrived_d)
    row, col = lax.axis_index("row"), lax.axis_index("col")
    me = row * cols_n + col
    plane, lane = col // width, col % width
    own_place = row * width + lane
    barrier = greet(sizes)

    def other_plane(k):
        return (plane // 2 + k // 2) % 2 * 2 + (plane % 2 + k % 2) % 2

    def neighbour_at(step):
        to_row, to_lane = (row + step // width) % rows_n, (lane + step % width) % width
        from_row = (row + rows_n - step // width) % rows_n
        from_lane = (lane + width - step % width) % width
        return (to_row, plane * width + to_lane), to_row, to_lane, from_row * width + from_lane

    def graph_copy(number, k, step, place):
        where, _, _, _ = neighbour_at(step)
        return pltpu.make_async_remote_copy(
            src_ref=sent.at[number * in_plane + step],
            dst_ref=arrived[number].at[pl.ds(place * (bucket * parts), bucket * parts)],
            send_sem=send_sem.at[number * in_plane + step],
            recv_sem=recv_sem.at[number * in_plane + step],
            device_id=where,
            device_id_type=MESH,
        )

    def relay_copy(number, k, to_plane, from_plane):
        return pltpu.make_async_remote_copy(
            src_ref=packed.at[number],
            dst_ref=unpacked.at[pl.ds(from_plane * units, units)],
            send_sem=relay_send_sem.at[number],
            recv_sem=relay_recv_sem.at[number],
            device_id=(row, to_plane * width + lane),
            device_id_type=MESH,
        )

    def terms_copy(step, target, slot):
        where, _, _ = partners(step, sizes)
        return pltpu.make_async_remote_copy(
            src_ref=terms.at[target],
            dst_ref=terms_in.at[slot],
            send_sem=terms_send_sem.at[step],
            recv_sem=terms_recv_sem.at[step],
            device_id=where,
            device_id_type=MESH,
        )

    node_rows = lax.broadcasted_iota(jnp.int32, (block, edges_ref.shape[2]), 0)
    node_index = lax.broadcasted_iota(jnp.int32, (block, hidden), 0)

    def compute(target, store):
        blends = []
        for j in range(bucket):
            graph = table_ref[target * bucket + j]
            features = features_ref[graph]
            edges = edges_ref[graph]
            sources = (node_rows == edges[0:1, :]).astype(jnp.float32).astype(jnp.bfloat16)
            targets = (node_rows == edges[1:2, :]).astype(jnp.float32).astype(jnp.bfloat16)
            adjacency = lax.dot_general(
                targets,
                sources,
                (((1,), (1,)), ((), ())),
                preferred_element_type=jnp.float32,
            ).astype(jnp.bfloat16)
            neighbour = jnp.dot(adjacency, features, preferred_element_type=jnp.float32)
            blends.append(
                (weight_ref[0] * features.astype(jnp.float32) + neighbour).astype(jnp.bfloat16)
            )
        blended = jnp.concatenate(blends, axis=0) if bucket > 1 else blends[0]
        hidden_one = jnp.maximum(
            jnp.dot(blended, w_first_ref[...], preferred_element_type=jnp.float32)
            + b_first_ref[...],
            0.0,
        ).astype(jnp.bfloat16)
        hidden_two = jnp.maximum(
            jnp.dot(hidden_one, w_second_ref[...], preferred_element_type=jnp.float32)
            + b_second_ref[...],
            0.0,
        ).astype(jnp.bfloat16)
        result = (
            jnp.dot(hidden_two, w_third_ref[...], preferred_element_type=jnp.float32)
            + b_third_ref[...]
        )
        for j in range(bucket):
            count = counts_ref[table_ref[target * bucket + j]]
            rows = jnp.where(node_index < count, result[j * block : (j + 1) * block], 0.0)
            rows = rows.astype(jnp.bfloat16)
            store(j, rows.reshape(parts, UNIT, hidden))
            total = jnp.sum(rows.astype(jnp.float32), axis=0, keepdims=True)
            pooled[target * bucket + j] = total / jnp.full((1, hidden), count).astype(jnp.float32)

    def first_stage(number, k):
        def compute_and_send(step, carry):
            _, to_row, to_lane, _ = neighbour_at(step)

            def store(j, rows):
                sent[number * in_plane + step, pl.ds(j * parts, parts)] = rows

            compute(to_row * cols_n + other_plane(k) * width + to_lane, store)
            graph_copy(number, k, step, own_place).start()
            return carry

        lax.fori_loop(1, in_plane, compute_and_send, 0)

        def store_own(j, rows):
            arrived[number][pl.ds((own_place * bucket + j) * parts, parts)] = rows

        compute(row * cols_n + other_plane(k) * width + lane, store_own)

    def second_stage(number, k):
        def finish(step, carry):
            _, _, _, source = neighbour_at(step)
            graph_copy(number, k, step, own_place).wait_send()
            graph_copy(number, k, step, source).wait_recv()
            return carry

        lax.fori_loop(1, in_plane, finish, 0)
        to_plane = other_plane(k)

        def pack(step, carry):
            for n in range(8):
                unit = step * 8 + n
                value = arrived[number][table_ref[pack_at + to_plane * units + unit]]
                if k == 0:
                    unpacked[plane * units + unit] = value
                else:
                    packed[number, unit] = value
            return carry

        lax.fori_loop(0, units // 8, pack, 0)
        if k != 0:
            relay_copy(number, k, to_plane, plane).start()

    pl.semaphore_wait(barrier, devices - 1)
    for number, k in enumerate(CLASSES):
        first_stage(number, k)
        if number > 0:
            second_stage(number - 1, CLASSES[number - 1])

    keys = lax.broadcasted_iota(jnp.int32, (devices * read_rows, slots), 0)
    members = (keys == ids_ref[...]).astype(jnp.float32)
    all_terms = jnp.dot(
        members,
        pooled[...].reshape(slots, hidden),
        precision=lax.Precision.HIGHEST,
        preferred_element_type=jnp.float32,
    )
    terms[...] = all_terms.reshape(devices, read_rows, hidden)

    def send_terms(step, carry):
        _, target, _ = partners(step, sizes)
        terms_copy(step, target, me).start()
        return carry

    lax.fori_loop(1, devices, send_terms, 0)
    terms_in[me] = terms[me]
    second_stage(PLANES - 1, CLASSES[PLANES - 1])

    def finish_terms(step, carry):
        _, target, source = partners(step, sizes)
        terms_copy(step, target, me).wait_send()
        terms_copy(step, target, source).wait_recv()
        return carry

    lax.fori_loop(1, devices, finish_terms, 0)
    readout_ref[...] = jnp.sum(terms_in[...], axis=0)
    for number, k in enumerate(CLASSES):
        if k != 0:
            relay_copy(number, k, other_plane(k), plane).wait_send()
            relay_copy(number, k, other_plane(k), other_plane(k)).wait_recv()

    def place(slot, carry):
        base = table_ref[base_at + slot]
        size = table_ref[size_at + slot]
        for part in range(parts):
            value = unpacked[jnp.minimum(base + part, PLANES * units - 1)]
            value = jnp.where(jnp.full((UNIT, hidden), size) > part, value, jnp.zeros_like(value))
            out_ref[slot, pl.ds(part * UNIT, UNIT), :] = value
        return carry

    lax.fori_loop(0, out_ref.shape[0], place, 0)


def body(
    sizes,
    node_features,
    node_counts,
    edge_list,
    readout_ids,
    live_graphs,
    self_weight,
    w_first,
    b_first,
    w_second,
    b_second,
    w_third,
    b_third,
):
    rows_n, cols_n = sizes
    devices = rows_n * cols_n
    width = cols_n // PLANES
    in_plane = rows_n * width
    capacity, block, hidden = node_features.shape
    parts = block // UNIT
    graphs_out = capacity // 2
    read_rows = 8
    bucket = (capacity + devices - 1) // devices
    slots_n = devices * bucket
    units = graphs_out * parts * 5 // (PLANES * 4)
    own_count = live_graphs[0]
    row, col = lax.axis_index("row"), lax.axis_index("col")
    plane, lane = col // width, col % width
    me = row * cols_n + col
    every = gather_counts(node_counts, live_graphs, sizes)
    every_count = every[:, capacity]
    earlier = jnp.arange(devices)[:, None] >= jnp.arange(devices)[None, :]
    inclusive = jnp.sum(jnp.where(earlier, every_count[None, :], 0), axis=1)
    offsets = inclusive - every_count
    offset = jnp.sum(jnp.where(jnp.arange(devices) == me, offsets, 0))
    slots = lax.broadcasted_iota(jnp.int32, (slots_n,), 0)
    within = (slots // bucket - offset) % devices + slots % bucket * devices
    picked = jnp.minimum(within, capacity - 1)
    choose = picked[:, None] == jnp.arange(capacity)[None, :]
    picked_ids = jnp.sum(jnp.where(choose, readout_ids[None, :], 0), axis=1)
    graph_ids = jnp.where(within < own_count, picked_ids, -1).reshape(1, -1)
    number = lax.broadcasted_iota(jnp.int32, (graphs_out,), 0) * devices + me
    passed = (inclusive[None, :] <= number[:, None]).astype(jnp.int32)
    source = jnp.sum(passed, axis=1)
    start = jnp.sum(passed * every_count[None, :], axis=1)
    turn = (number - start) // devices

    index = jnp.arange(capacity)[None, :]
    sizes_all = jnp.where(
        index < every_count[:, None], (every[:, :capacity] + (UNIT - 1)) // UNIT, 0
    )
    dests = (offsets[:, None] + index) % devices
    by_dest = jnp.sum(
        jnp.where(dests[:, :, None] == jnp.arange(devices), sizes_all[:, :, None], 0), axis=1
    )
    plane_load = jnp.sum(by_dest.reshape(rows_n, PLANES, width, devices), axis=(0, 2))
    fits = jnp.max(plane_load) <= units

    turns = jnp.arange(bucket)[:, None] == index // devices

    def by_plane(values):
        values = values.reshape(rows_n, PLANES, width, capacity)
        return jnp.swapaxes(values, 0, 1).reshape(PLANES, in_plane, capacity)

    plane_sizes, plane_dests = by_plane(sizes_all), by_plane(dests)
    own_sizes = lax.dynamic_index_in_dim(plane_sizes, plane, 0, keepdims=False)
    own_dests = lax.dynamic_index_in_dim(plane_dests, plane, 0, keepdims=False)

    def slot_sizes(values, wanted):
        chosen = wanted[:, :, None, :] & turns
        return jnp.sum(jnp.where(chosen, values[:, :, None, :], 0), axis=3).reshape(PLANES, -1)

    relay_dests = row * cols_n + jnp.arange(PLANES) * width + lane
    relay_sizes = slot_sizes(own_sizes[None], own_dests[None] == relay_dests[:, None, None])
    final_sizes = slot_sizes(plane_sizes, plane_dests == me)
    places = in_plane * bucket
    before = jnp.arange(places)[:, None] >= jnp.arange(places)[None, :]

    def ends(values):
        return jnp.sum(jnp.where(before, values[:, None, :], 0), axis=2)

    done = ends(relay_sizes)[:, None, :] <= jnp.arange(units)[None, :, None]
    slot_of = jnp.minimum(jnp.sum(done.astype(jnp.int32), axis=2), places - 1)
    part_of = jnp.arange(units) - jnp.sum(jnp.where(done, relay_sizes[:, None, :], 0), axis=2)
    pack = slot_of * parts + jnp.clip(part_of, 0, parts - 1)
    starts = ends(final_sizes) - final_sizes + jnp.arange(PLANES)[:, None] * units
    source_row, source_col = source // cols_n, source % cols_n
    place = (source_row * width + source_col % width) * bucket + turn
    place = source_col // width * places + place
    match = place[:, None] == jnp.arange(PLANES * places)[None, :]
    base = jnp.sum(jnp.where(match, starts.reshape(1, -1), 0), axis=1)
    size = jnp.sum(jnp.where(match, final_sizes.reshape(1, -1), 0), axis=1)
    table = jnp.concatenate([picked, pack.reshape(-1), base, size]).astype(jnp.int32)
    arrival = (source * bucket + turn).astype(jnp.int32)

    out_shape = (
        jax.ShapeDtypeStruct((graphs_out, block, hidden), jnp.bfloat16),
        jax.ShapeDtypeStruct((read_rows, hidden), jnp.float32),
    )
    pooled_scratch = [
        pltpu.VMEM((slots_n, 1, hidden), jnp.float32),
        pltpu.VMEM((devices, read_rows, hidden), jnp.float32),
        pltpu.VMEM((devices, read_rows, hidden), jnp.float32),
    ]

    def semaphores(count):
        return [pltpu.SemaphoreType.DMA((count,)), pltpu.SemaphoreType.DMA((count,))]

    def relayed(*operands):
        table, _, node_counts = operands[:3]
        graphs = pltpu.VMEM((in_plane * bucket * parts, UNIT, hidden), jnp.bfloat16)
        return pl.pallas_call(
            functools.partial(relay_kernel, sizes, bucket, units),
            out_shape=out_shape,
            in_specs=[SMEM] * 3 + [VMEM] * 9,
            out_specs=(VMEM, VMEM),
            scratch_shapes=[
                pltpu.VMEM((devices, bucket * parts, UNIT, hidden), jnp.bfloat16),
                graphs,
                graphs,
                graphs,
                graphs,
                pltpu.VMEM((PLANES - 1, units, UNIT, hidden), jnp.bfloat16),
                pltpu.VMEM((PLANES * units, UNIT, hidden), jnp.bfloat16),
            ]
            + pooled_scratch
            + semaphores(devices)
            + semaphores(PLANES)
            + semaphores(devices),
            compiler_params=pltpu.CompilerParams(
                collective_id=2, has_side_effects=True, vmem_limit_bytes=61 * 1024 * 1024
            ),
            name="gin_relay",
        )(table, node_counts, *operands[3:])

    def direct(*operands):
        table, arrival, node_counts = operands[:3]
        graphs = pltpu.VMEM((devices, bucket, block, hidden), jnp.bfloat16)
        return pl.pallas_call(
            functools.partial(layer_kernel, sizes, bucket),
            out_shape=out_shape,
            in_specs=[SMEM] * 4 + [VMEM] * 9,
            out_specs=(VMEM, VMEM),
            scratch_shapes=[graphs, graphs]
            + pooled_scratch
            + semaphores(devices)
            + semaphores(devices),
            compiler_params=pltpu.CompilerParams(
                collective_id=1, has_side_effects=True, vmem_limit_bytes=60 * 1024 * 1024
            ),
            name="gin_direct",
        )(table[:slots_n], node_counts, arrival, *operands[3:])

    return lax.cond(
        fits,
        relayed,
        direct,
        table,
        arrival,
        node_counts,
        self_weight,
        node_features,
        edge_list,
        graph_ids,
        w_first,
        b_first.reshape(1, -1),
        w_second,
        b_second.reshape(1, -1),
        w_third,
        b_third.reshape(1, -1),
    )


def solution(mesh):
    sizes = (mesh.shape["row"], mesh.shape["col"])
    both = ("row", "col")
    in_specs = (
        P(both, None, None),
        P(both),
        P(both, None, None),
        P(both),
        P(both),
        P(),
        P(),
        P(),
        P(),
        P(),
        P(),
        P(),
    )
    out_specs = (P(both, None, None), P(both, None))
    return jax.shard_map(
        functools.partial(body, sizes),
        mesh=mesh,
        in_specs=in_specs,
        out_specs=out_specs,
        check_vma=False,
    )
```

```python
import functools

import jax
import jax.numpy as jnp
from jax import lax
from jax.experimental import pallas as pl
from jax.experimental.pallas import tpu as pltpu
from jax.sharding import PartitionSpec as P

MESH = pl.DeviceIdType.MESH
VMEM = pl.BlockSpec(memory_space=pltpu.VMEM)
SMEM = pl.BlockSpec(memory_space=pltpu.SMEM)
HBM = pl.BlockSpec(memory_space=pltpu.HBM)
PLANES = 4
UNIT = 16
CLASSES = (2, 3, 1, 0)


def partners(step, sizes):
    rows, cols = sizes
    row, col = lax.axis_index("row"), lax.axis_index("col")
    by_row, by_col = step // cols, (step % cols) * 3 % cols
    to_row, to_col = (row + by_row) % rows, (col + by_col) % cols
    from_row, from_col = (row + rows - by_row) % rows, (col + cols - by_col) % cols
    return (to_row, to_col), to_row * cols + to_col, from_row * cols + from_col


def greet(sizes):
    barrier = pltpu.get_barrier_semaphore()
    devices = sizes[0] * sizes[1]

    def signal(step, carry):
        where, _, _ = partners(step, sizes)
        pl.semaphore_signal(barrier, inc=1, device_id=where, device_id_type=MESH)
        return carry

    lax.fori_loop(1, devices, signal, 0)
    return barrier


def gather_kernel(sizes, own_ref, all_ref, send_sem, recv_sem):
    devices = sizes[0] * sizes[1]
    me = lax.axis_index("row") * sizes[1] + lax.axis_index("col")
    barrier = greet(sizes)
    all_ref[me] = own_ref[0]
    pl.semaphore_wait(barrier, devices - 1)

    def copy(step, slot):
        where, _, _ = partners(step, sizes)
        return pltpu.make_async_remote_copy(
            src_ref=own_ref.at[0],
            dst_ref=all_ref.at[slot],
            send_sem=send_sem.at[step],
            recv_sem=recv_sem.at[step],
            device_id=where,
            device_id_type=MESH,
        )

    def send(step, carry):
        copy(step, me).start()
        return carry

    def finish(step, carry):
        _, _, source = partners(step, sizes)
        copy(step, me).wait_send()
        copy(step, source).wait_recv()
        return carry

    lax.fori_loop(1, devices, send, 0)
    lax.fori_loop(1, devices, finish, 0)


def gather_counts(node_counts, live_graphs, sizes):
    devices = sizes[0] * sizes[1]
    own = jnp.concatenate([node_counts, live_graphs])
    own = jnp.pad(own, (0, -own.shape[0] % 128)).reshape(1, 1, -1)
    every = pl.pallas_call(
        functools.partial(gather_kernel, sizes),
        out_shape=jax.ShapeDtypeStruct((devices, 1, own.shape[2]), jnp.int32),
        in_specs=[VMEM],
        out_specs=VMEM,
        scratch_shapes=[
            pltpu.SemaphoreType.DMA((devices,)),
            pltpu.SemaphoreType.DMA((devices,)),
        ],
        compiler_params=pltpu.CompilerParams(collective_id=0, has_side_effects=True),
        name="gather_counts",
    )(own)
    return every[:, 0, :]


def layer_kernel(
    sizes,
    bucket,
    picked_ref,
    counts_ref,
    arrival_ref,
    weight_ref,
    features_ref,
    edges_ref,
    ids_ref,
    w_first_ref,
    b_first_ref,
    w_second_ref,
    b_second_ref,
    w_third_ref,
    b_third_ref,
    out_ref,
    readout_ref,
    sent,
    arrived,
    pooled,
    terms,
    terms_in,
    send_sem,
    recv_sem,
    terms_send_sem,
    terms_recv_sem,
):
    devices = sizes[0] * sizes[1]
    read_rows = readout_ref.shape[0]
    block, hidden = features_ref.shape[1:]
    me = lax.axis_index("row") * sizes[1] + lax.axis_index("col")
    barrier = greet(sizes)

    def graph_copy(step, target, slot):
        where, _, _ = partners(step, sizes)
        return pltpu.make_async_remote_copy(
            src_ref=sent.at[target],
            dst_ref=arrived.at[slot],
            send_sem=send_sem.at[step],
            recv_sem=recv_sem.at[step],
            device_id=where,
            device_id_type=MESH,
        )

    def terms_copy(step, target, slot):
        where, _, _ = partners(step, sizes)
        return pltpu.make_async_remote_copy(
            src_ref=terms.at[target],
            dst_ref=terms_in.at[slot],
            send_sem=terms_send_sem.at[step],
            recv_sem=terms_recv_sem.at[step],
            device_id=where,
            device_id_type=MESH,
        )

    node_rows = lax.broadcasted_iota(jnp.int32, (block, edges_ref.shape[2]), 0)
    node_index = lax.broadcasted_iota(jnp.int32, (block, hidden), 0)

    def compute(target, store):
        blends = []
        for j in range(bucket):
            graph = picked_ref[target * bucket + j]
            features = features_ref[graph]
            edges = edges_ref[graph]
            sources = (node_rows == edges[0:1, :]).astype(jnp.float32).astype(jnp.bfloat16)
            targets = (node_rows == edges[1:2, :]).astype(jnp.float32).astype(jnp.bfloat16)
            adjacency = lax.dot_general(
                targets,
                sources,
                (((1,), (1,)), ((), ())),
                preferred_element_type=jnp.float32,
            ).astype(jnp.bfloat16)
            neighbour = jnp.dot(adjacency, features, preferred_element_type=jnp.float32)
            blends.append(
                (weight_ref[0] * features.astype(jnp.float32) + neighbour).astype(jnp.bfloat16)
            )
        blended = jnp.concatenate(blends, axis=0) if bucket > 1 else blends[0]
        hidden_one = jnp.maximum(
            jnp.dot(blended, w_first_ref[...], preferred_element_type=jnp.float32)
            + b_first_ref[...],
            0.0,
        ).astype(jnp.bfloat16)
        hidden_two = jnp.maximum(
            jnp.dot(hidden_one, w_second_ref[...], preferred_element_type=jnp.float32)
            + b_second_ref[...],
            0.0,
        ).astype(jnp.bfloat16)
        result = (
            jnp.dot(hidden_two, w_third_ref[...], preferred_element_type=jnp.float32)
            + b_third_ref[...]
        )
        for j in range(bucket):
            count = counts_ref[picked_ref[target * bucket + j]]
            rows = jnp.where(node_index < count, result[j * block : (j + 1) * block], 0.0)
            rows = rows.astype(jnp.bfloat16)
            store(j, rows)
            total = jnp.sum(rows.astype(jnp.float32), axis=0, keepdims=True)
            pooled[target * bucket + j] = total / jnp.full((1, hidden), count).astype(jnp.float32)

    pl.semaphore_wait(barrier, devices - 1)

    def compute_and_send(step, carry):
        _, target, _ = partners(step, sizes)

        def store(j, rows):
            sent[target, j] = rows

        compute(target, store)
        graph_copy(step, target, me).start()
        return carry

    lax.fori_loop(1, devices, compute_and_send, 0)

    def store_own(j, rows):
        arrived[me, j] = rows

    compute(me, store_own)

    slots = devices * bucket
    keys = lax.broadcasted_iota(jnp.int32, (devices * read_rows, slots), 0)
    members = (keys == ids_ref[...]).astype(jnp.float32)
    all_terms = jnp.dot(
        members,
        pooled[...].reshape(slots, hidden),
        precision=lax.Precision.HIGHEST,
        preferred_element_type=jnp.float32,
    )
    terms[...] = all_terms.reshape(devices, read_rows, hidden)

    def send_terms(step, carry):
        _, target, _ = partners(step, sizes)
        terms_copy(step, target, me).start()
        return carry

    lax.fori_loop(1, devices, send_terms, 0)
    terms_in[me] = terms[me]

    def finish(step, carry):
        _, target, source = partners(step, sizes)
        graph_copy(step, target, me).wait_send()
        graph_copy(step, target, source).wait_recv()
        terms_copy(step, target, me).wait_send()
        terms_copy(step, target, source).wait_recv()
        return carry

    lax.fori_loop(1, devices, finish, 0)
    readout_ref[...] = jnp.sum(terms_in[...], axis=0)

    def place(slot, carry):
        which = arrival_ref[slot]
        out_ref[slot] = arrived[which // bucket, which % bucket]
        return carry

    lax.fori_loop(0, out_ref.shape[0], place, 0)


def relay_kernel(
    sizes,
    bucket,
    units,
    most_units,
    table_ref,
    counts_ref,
    weight_ref,
    features_ref,
    edges_ref,
    ids_ref,
    w_first_ref,
    b_first_ref,
    w_second_ref,
    b_second_ref,
    w_third_ref,
    b_third_ref,
    out_ref,
    readout_ref,
    sent,
    arrived_a,
    arrived_b,
    arrived_c,
    arrived_d,
    packed,
    unpacked,
    pooled,
    terms,
    terms_in,
    plane_terms,
    final_terms,
    send_sem,
    recv_sem,
    relay_send_sem,
    relay_recv_sem,
    terms_send_sem,
    terms_recv_sem,
    final_send_sem,
    final_recv_sem,
    out_sem,
):
    rows_n, cols_n = sizes
    devices = rows_n * cols_n
    width = cols_n // PLANES
    in_plane = rows_n * width
    read_rows = readout_ref.shape[0]
    block, hidden = features_ref.shape[1:]
    parts = block // UNIT
    slots = devices * bucket
    pack_at = slots
    base_at = pack_at + PLANES * most_units
    size_at = base_at + out_ref.shape[0]
    plane_at = size_at + out_ref.shape[0]
    arrived = (arrived_a, arrived_b, arrived_c, arrived_d)
    row, col = lax.axis_index("row"), lax.axis_index("col")
    me = row * cols_n + col
    plane, lane = col // width, col % width
    own_place = row * width + lane
    barrier = greet(sizes)

    def other_plane(k):
        return (plane // 2 + k // 2) % 2 * 2 + (plane % 2 + k % 2) % 2

    def neighbour_at(step):
        to_row, to_lane = (row + step // width) % rows_n, (lane + step % width) % width
        from_row = (row + rows_n - step // width) % rows_n
        from_lane = (lane + width - step % width) % width
        return (to_row, plane * width + to_lane), to_row, to_lane, from_row * width + from_lane

    def graph_copy(number, k, step, place):
        where, _, _, _ = neighbour_at(step)
        return pltpu.make_async_remote_copy(
            src_ref=sent.at[number * in_plane + step],
            dst_ref=arrived[number].at[pl.ds(place * (bucket * parts), bucket * parts)],
            send_sem=send_sem.at[number * in_plane + step],
            recv_sem=recv_sem.at[number * in_plane + step],
            device_id=where,
            device_id_type=MESH,
        )

    def relay_copy(number, k, to_plane, from_plane):
        return pltpu.make_async_remote_copy(
            src_ref=packed.at[number],
            dst_ref=unpacked.at[pl.ds(from_plane * units, units)],
            send_sem=relay_send_sem.at[number],
            recv_sem=relay_recv_sem.at[number],
            device_id=(row, to_plane * width + lane),
            device_id_type=MESH,
        )

    def terms_copy(step, target, slot):
        where, _, _, _ = neighbour_at(step)
        return pltpu.make_async_remote_copy(
            src_ref=terms.at[target],
            dst_ref=terms_in.at[slot],
            send_sem=terms_send_sem.at[step],
            recv_sem=terms_recv_sem.at[step],
            device_id=where,
            device_id_type=MESH,
        )

    def final_copy(number, to_plane, from_plane):
        return pltpu.make_async_remote_copy(
            src_ref=plane_terms.at[to_plane],
            dst_ref=final_terms.at[from_plane],
            send_sem=final_send_sem.at[number],
            recv_sem=final_recv_sem.at[number],
            device_id=(row, to_plane * width + lane),
            device_id_type=MESH,
        )

    node_rows = lax.broadcasted_iota(jnp.int32, (block, edges_ref.shape[2]), 0)
    node_index = lax.broadcasted_iota(jnp.int32, (block, hidden), 0)

    def compute(target, store):
        blends = []
        for j in range(bucket):
            graph = table_ref[target * bucket + j]
            features = features_ref[graph]
            edges = edges_ref[graph]
            sources = (node_rows == edges[0:1, :]).astype(jnp.float32).astype(jnp.bfloat16)
            targets = (node_rows == edges[1:2, :]).astype(jnp.float32).astype(jnp.bfloat16)
            adjacency = lax.dot_general(
                targets,
                sources,
                (((1,), (1,)), ((), ())),
                preferred_element_type=jnp.float32,
            ).astype(jnp.bfloat16)
            neighbour = jnp.dot(adjacency, features, preferred_element_type=jnp.float32)
            blends.append(
                (weight_ref[0] * features.astype(jnp.float32) + neighbour).astype(jnp.bfloat16)
            )
        blended = jnp.concatenate(blends, axis=0) if bucket > 1 else blends[0]
        hidden_one = jnp.maximum(
            jnp.dot(blended, w_first_ref[...], preferred_element_type=jnp.float32)
            + b_first_ref[...],
            0.0,
        ).astype(jnp.bfloat16)
        hidden_two = jnp.maximum(
            jnp.dot(hidden_one, w_second_ref[...], preferred_element_type=jnp.float32)
            + b_second_ref[...],
            0.0,
        ).astype(jnp.bfloat16)
        result = (
            jnp.dot(hidden_two, w_third_ref[...], preferred_element_type=jnp.float32)
            + b_third_ref[...]
        )
        for j in range(bucket):
            count = counts_ref[table_ref[target * bucket + j]]
            rows = jnp.where(node_index < count, result[j * block : (j + 1) * block], 0.0)
            rows = rows.astype(jnp.bfloat16)
            store(j, rows.reshape(parts, UNIT, hidden))
            total = jnp.sum(rows.astype(jnp.float32), axis=0, keepdims=True)
            pooled[target * bucket + j] = total / jnp.full((1, hidden), count).astype(jnp.float32)

    def first_stage(number, k, lower, upper):
        def compute_and_send(step, carry):
            _, to_row, to_lane, _ = neighbour_at(step)

            def store(j, rows):
                sent[number * in_plane + step, pl.ds(j * parts, parts)] = rows

            compute(to_row * cols_n + other_plane(k) * width + to_lane, store)
            graph_copy(number, k, step, own_place).start()
            return carry

        lax.fori_loop(lower, upper, compute_and_send, 0)
        if upper < in_plane:
            return

        def store_own(j, rows):
            arrived[number][pl.ds((own_place * bucket + j) * parts, parts)] = rows

        compute(row * cols_n + other_plane(k) * width + lane, store_own)

    def second_stage(number, k):
        def finish(step, carry):
            _, _, _, source = neighbour_at(step)
            graph_copy(number, k, step, own_place).wait_send()
            graph_copy(number, k, step, source).wait_recv()
            return carry

        lax.fori_loop(1, in_plane, finish, 0)
        to_plane = other_plane(k)

        def pack(step, carry):
            for n in range(8):
                unit = step * 8 + n
                value = arrived[number][table_ref[pack_at + to_plane * most_units + unit]]
                if k == 0:
                    unpacked[plane * units + unit] = value
                else:
                    packed[number, unit] = value
            return carry

        lax.fori_loop(0, units // 8, pack, 0)
        if k != 0:
            relay_copy(number, k, to_plane, plane).start()

    pl.semaphore_wait(barrier, devices - 1)
    for number, k in enumerate(CLASSES):
        if number == 1:
            first_stage(number, k, 1, in_plane // 2)
            second_stage(0, CLASSES[0])
            first_stage(number, k, in_plane // 2, in_plane)
        else:
            first_stage(number, k, 1, in_plane)
        if number > 1:
            second_stage(number - 1, CLASSES[number - 1])

    keys = lax.broadcasted_iota(jnp.int32, (devices * read_rows, slots), 0)
    members = (keys == ids_ref[...]).astype(jnp.float32)
    all_terms = jnp.dot(
        members,
        pooled[...].reshape(slots, hidden),
        precision=lax.Precision.HIGHEST,
        preferred_element_type=jnp.float32,
    )
    for place in range(in_plane):
        for to_plane in range(PLANES):
            device = place // width * cols_n + to_plane * width + place % width
            terms[place, to_plane] = all_terms[device * read_rows : (device + 1) * read_rows]

    def send_terms(step, carry):
        _, to_row, to_lane, _ = neighbour_at(step)
        terms_copy(step, to_row * width + to_lane, own_place).start()
        return carry

    lax.fori_loop(1, in_plane, send_terms, 0)
    terms_in[own_place] = terms[own_place]
    second_stage(PLANES - 1, CLASSES[PLANES - 1])

    def finish_terms(step, carry):
        _, to_row, to_lane, source = neighbour_at(step)
        terms_copy(step, to_row * width + to_lane, own_place).wait_send()
        terms_copy(step, to_row * width + to_lane, source).wait_recv()
        return carry

    lax.fori_loop(1, in_plane, finish_terms, 0)
    plane_terms[...] = jnp.sum(terms_in[...], axis=0)
    final_terms[plane] = plane_terms[plane]
    for number, k in enumerate(CLASSES):
        if k != 0:
            final_copy(number, other_plane(k), plane).start()
    for number, k in enumerate(CLASSES):
        if k != 0:
            relay_copy(number, k, other_plane(k), plane).wait_send()
            relay_copy(number, k, other_plane(k), other_plane(k)).wait_recv()

    def out_copy(slot):
        return pltpu.make_async_copy(
            sent.at[slot // bucket, pl.ds(slot % bucket * parts, parts)],
            out_ref.at[slot],
            out_sem.at[slot],
        )

    def place_graph(slot, carry):
        base = table_ref[base_at + slot] + table_ref[plane_at + slot] * units
        size = table_ref[size_at + slot]
        for part in range(parts):
            value = unpacked[jnp.minimum(base + part, PLANES * units - 1)]
            value = jnp.where(jnp.full((UNIT, hidden), size) > part, value, jnp.zeros_like(value))
            sent[slot // bucket, slot % bucket * parts + part] = value
        out_copy(slot).start()
        return carry

    lax.fori_loop(0, out_ref.shape[0], place_graph, 0)
    for number, k in enumerate(CLASSES):
        if k != 0:
            final_copy(number, other_plane(k), plane).wait_send()
            final_copy(number, other_plane(k), other_plane(k)).wait_recv()
    readout_ref[...] = jnp.sum(final_terms[...], axis=0)

    def finish_out(slot, carry):
        out_copy(slot).wait()
        return carry

    lax.fori_loop(0, out_ref.shape[0], finish_out, 0)


def body(
    sizes,
    node_features,
    node_counts,
    edge_list,
    readout_ids,
    live_graphs,
    self_weight,
    w_first,
    b_first,
    w_second,
    b_second,
    w_third,
    b_third,
):
    rows_n, cols_n = sizes
    devices = rows_n * cols_n
    width = cols_n // PLANES
    in_plane = rows_n * width
    capacity, block, hidden = node_features.shape
    parts = block // UNIT
    graphs_out = capacity // 2
    read_rows = 8
    bucket = (capacity + devices - 1) // devices
    slots_n = devices * bucket
    mean_units = graphs_out * parts // PLANES
    caps = [mean_units * eighths // 64 * 8 for eighths in (8, 9, 11)]
    units = caps[-1]
    own_count = live_graphs[0]
    row, col = lax.axis_index("row"), lax.axis_index("col")
    plane, lane = col // width, col % width
    me = row * cols_n + col
    every = gather_counts(node_counts, live_graphs, sizes)
    every_count = every[:, capacity]
    earlier = jnp.arange(devices)[:, None] >= jnp.arange(devices)[None, :]
    inclusive = jnp.sum(jnp.where(earlier, every_count[None, :], 0), axis=1)
    offsets = inclusive - every_count
    offset = jnp.sum(jnp.where(jnp.arange(devices) == me, offsets, 0))
    slots = lax.broadcasted_iota(jnp.int32, (slots_n,), 0)
    within = (slots // bucket - offset) % devices + slots % bucket * devices
    picked = jnp.minimum(within, capacity - 1)
    choose = picked[:, None] == jnp.arange(capacity)[None, :]
    picked_ids = jnp.sum(jnp.where(choose, readout_ids[None, :], 0), axis=1)
    graph_ids = jnp.where(within < own_count, picked_ids, -1).reshape(1, -1)
    number = lax.broadcasted_iota(jnp.int32, (graphs_out,), 0) * devices + me
    passed = (inclusive[None, :] <= number[:, None]).astype(jnp.int32)
    source = jnp.sum(passed, axis=1)
    start = jnp.sum(passed * every_count[None, :], axis=1)
    turn = (number - start) // devices

    index = jnp.arange(capacity)[None, :]
    sizes_all = jnp.where(
        index < every_count[:, None], (every[:, :capacity] + (UNIT - 1)) // UNIT, 0
    )
    dests = (offsets[:, None] + index) % devices
    by_dest = jnp.sum(
        jnp.where(dests[:, :, None] == jnp.arange(devices), sizes_all[:, :, None], 0), axis=1
    )
    plane_load = jnp.sum(by_dest.reshape(rows_n, PLANES, width, devices), axis=(0, 2))
    most = jnp.max(plane_load)
    tier = sum((most > cap).astype(jnp.int32) for cap in caps)

    turns = jnp.arange(bucket)[:, None] == index // devices

    def by_plane(values):
        values = values.reshape(rows_n, PLANES, width, capacity)
        return jnp.swapaxes(values, 0, 1).reshape(PLANES, in_plane, capacity)

    plane_sizes, plane_dests = by_plane(sizes_all), by_plane(dests)
    own_sizes = lax.dynamic_index_in_dim(plane_sizes, plane, 0, keepdims=False)
    own_dests = lax.dynamic_index_in_dim(plane_dests, plane, 0, keepdims=False)

    def slot_sizes(values, wanted):
        chosen = wanted[:, :, None, :] & turns
        return jnp.sum(jnp.where(chosen, values[:, :, None, :], 0), axis=3).reshape(PLANES, -1)

    relay_dests = row * cols_n + jnp.arange(PLANES) * width + lane
    relay_sizes = slot_sizes(own_sizes[None], own_dests[None] == relay_dests[:, None, None])
    final_sizes = slot_sizes(plane_sizes, plane_dests == me)
    places = in_plane * bucket
    before = jnp.arange(places)[:, None] >= jnp.arange(places)[None, :]

    def ends(values):
        return jnp.sum(jnp.where(before, values[:, None, :], 0), axis=2)

    done = ends(relay_sizes)[:, None, :] <= jnp.arange(units)[None, :, None]
    slot_of = jnp.minimum(jnp.sum(done.astype(jnp.int32), axis=2), places - 1)
    part_of = jnp.arange(units) - jnp.sum(jnp.where(done, relay_sizes[:, None, :], 0), axis=2)
    pack = slot_of * parts + jnp.clip(part_of, 0, parts - 1)
    starts = ends(final_sizes) - final_sizes
    source_row, source_col = source // cols_n, source % cols_n
    place = (source_row * width + source_col % width) * bucket + turn
    place = source_col // width * places + place
    match = place[:, None] == jnp.arange(PLANES * places)[None, :]
    base = jnp.sum(jnp.where(match, starts.reshape(1, -1), 0), axis=1)
    size = jnp.sum(jnp.where(match, final_sizes.reshape(1, -1), 0), axis=1)
    table = jnp.concatenate([picked, pack.reshape(-1), base, size, source_col // width]).astype(jnp.int32)
    arrival = (source * bucket + turn).astype(jnp.int32)

    out_shape = (
        jax.ShapeDtypeStruct((graphs_out, block, hidden), jnp.bfloat16),
        jax.ShapeDtypeStruct((read_rows, hidden), jnp.float32),
    )
    pooled_scratch = pltpu.VMEM((slots_n, 1, hidden), jnp.float32)

    def semaphores(count):
        return [pltpu.SemaphoreType.DMA((count,)), pltpu.SemaphoreType.DMA((count,))]

    def relayed(tier, units, *operands):
        table, _, node_counts = operands[:3]
        graphs = pltpu.VMEM((in_plane * bucket * parts, UNIT, hidden), jnp.bfloat16)
        whole_terms = pltpu.VMEM((in_plane, PLANES, read_rows, hidden), jnp.float32)
        some_terms = pltpu.VMEM((PLANES, read_rows, hidden), jnp.float32)
        node_out, readout = pl.pallas_call(
            functools.partial(relay_kernel, sizes, bucket, units, caps[-1]),
            out_shape=(
                jax.ShapeDtypeStruct((graphs_out, parts, UNIT, hidden), jnp.bfloat16),
                out_shape[1],
            ),
            in_specs=[SMEM] * 3 + [VMEM] * 9,
            out_specs=(HBM, VMEM),
            scratch_shapes=[
                pltpu.VMEM((devices, bucket * parts, UNIT, hidden), jnp.bfloat16),
                graphs,
                graphs,
                graphs,
                graphs,
                pltpu.VMEM((PLANES - 1, units, UNIT, hidden), jnp.bfloat16),
                pltpu.VMEM((PLANES * units, UNIT, hidden), jnp.bfloat16),
            ]
            + [pooled_scratch, whole_terms, whole_terms, some_terms, some_terms]
            + semaphores(devices)
            + semaphores(PLANES)
            + semaphores(in_plane)
            + semaphores(PLANES)
            + [pltpu.SemaphoreType.DMA((graphs_out,))],
            compiler_params=pltpu.CompilerParams(
                collective_id=2 + tier, has_side_effects=True, vmem_limit_bytes=61 * 1024 * 1024
            ),
            name="gin_relay",
        )(table, node_counts, *operands[3:])
        return node_out.reshape(graphs_out, block, hidden), readout

    def direct(*operands):
        table, arrival, node_counts = operands[:3]
        all_terms = pltpu.VMEM((devices, read_rows, hidden), jnp.float32)
        graphs = pltpu.VMEM((devices, bucket, block, hidden), jnp.bfloat16)
        return pl.pallas_call(
            functools.partial(layer_kernel, sizes, bucket),
            out_shape=out_shape,
            in_specs=[SMEM] * 4 + [VMEM] * 9,
            out_specs=(VMEM, VMEM),
            scratch_shapes=[graphs, graphs]
            + [pooled_scratch, all_terms, all_terms]
            + semaphores(devices)
            + semaphores(devices),
            compiler_params=pltpu.CompilerParams(
                collective_id=1, has_side_effects=True, vmem_limit_bytes=60 * 1024 * 1024
            ),
            name="gin_direct",
        )(table[:slots_n], node_counts, arrival, *operands[3:])

    branches = [functools.partial(relayed, number, cap) for number, cap in enumerate(caps)]
    return lax.switch(
        tier,
        branches + [direct],
        table,
        arrival,
        node_counts,
        self_weight,
        node_features,
        edge_list,
        graph_ids,
        w_first,
        b_first.reshape(1, -1),
        w_second,
        b_second.reshape(1, -1),
        w_third,
        b_third.reshape(1, -1),
    )


def solution(mesh):
    sizes = (mesh.shape["row"], mesh.shape["col"])
    both = ("row", "col")
    in_specs = (
        P(both, None, None),
        P(both),
        P(both, None, None),
        P(both),
        P(both),
        P(),
        P(),
        P(),
        P(),
        P(),
        P(),
        P(),
    )
    out_specs = (P(both, None, None), P(both, None))
    return jax.shard_map(
        functools.partial(body, sizes),
        mesh=mesh,
        in_specs=in_specs,
        out_specs=out_specs,
        check_vma=False,
    )
```

```python
import functools

import jax
import jax.numpy as jnp
from jax import lax
from jax.experimental import pallas as pl
from jax.experimental.pallas import tpu as pltpu
from jax.sharding import PartitionSpec as P

MESH = pl.DeviceIdType.MESH
VMEM = pl.BlockSpec(memory_space=pltpu.VMEM)
SMEM = pl.BlockSpec(memory_space=pltpu.SMEM)
HBM = pl.BlockSpec(memory_space=pltpu.HBM)
PLANES = 4
UNIT = 16
CLASSES = (2, 3, 1, 0)


def partners(step, sizes):
    rows, cols = sizes
    row, col = lax.axis_index("row"), lax.axis_index("col")
    by_row, by_col = step // cols, (step % cols) * 3 % cols
    to_row, to_col = (row + by_row) % rows, (col + by_col) % cols
    from_row, from_col = (row + rows - by_row) % rows, (col + cols - by_col) % cols
    return (to_row, to_col), to_row * cols + to_col, from_row * cols + from_col


def greet(sizes):
    barrier = pltpu.get_barrier_semaphore()
    devices = sizes[0] * sizes[1]

    def signal(step, carry):
        where, _, _ = partners(step, sizes)
        pl.semaphore_signal(barrier, inc=1, device_id=where, device_id_type=MESH)
        return carry

    lax.fori_loop(1, devices, signal, 0)
    return barrier


def gather_kernel(sizes, own_ref, all_ref, send_sem, recv_sem):
    devices = sizes[0] * sizes[1]
    me = lax.axis_index("row") * sizes[1] + lax.axis_index("col")
    barrier = greet(sizes)
    all_ref[me] = own_ref[0]
    pl.semaphore_wait(barrier, devices - 1)

    def copy(step, slot):
        where, _, _ = partners(step, sizes)
        return pltpu.make_async_remote_copy(
            src_ref=own_ref.at[0],
            dst_ref=all_ref.at[slot],
            send_sem=send_sem.at[step],
            recv_sem=recv_sem.at[step],
            device_id=where,
            device_id_type=MESH,
        )

    def send(step, carry):
        copy(step, me).start()
        return carry

    def finish(step, carry):
        _, _, source = partners(step, sizes)
        copy(step, me).wait_send()
        copy(step, source).wait_recv()
        return carry

    lax.fori_loop(1, devices, send, 0)
    lax.fori_loop(1, devices, finish, 0)


def gather_counts(node_counts, live_graphs, sizes):
    devices = sizes[0] * sizes[1]
    own = jnp.concatenate([node_counts, live_graphs])
    own = jnp.pad(own, (0, -own.shape[0] % 128)).reshape(1, 1, -1)
    every = pl.pallas_call(
        functools.partial(gather_kernel, sizes),
        out_shape=jax.ShapeDtypeStruct((devices, 1, own.shape[2]), jnp.int32),
        in_specs=[VMEM],
        out_specs=VMEM,
        scratch_shapes=[
            pltpu.SemaphoreType.DMA((devices,)),
            pltpu.SemaphoreType.DMA((devices,)),
        ],
        compiler_params=pltpu.CompilerParams(collective_id=0, has_side_effects=True),
        name="gather_counts",
    )(own)
    return every[:, 0, :]


def layer_kernel(
    sizes,
    bucket,
    picked_ref,
    counts_ref,
    arrival_ref,
    weight_ref,
    features_ref,
    edges_ref,
    ids_ref,
    w_first_ref,
    b_first_ref,
    w_second_ref,
    b_second_ref,
    w_third_ref,
    b_third_ref,
    out_ref,
    readout_ref,
    sent,
    arrived,
    pooled,
    terms,
    terms_in,
    send_sem,
    recv_sem,
    terms_send_sem,
    terms_recv_sem,
):
    devices = sizes[0] * sizes[1]
    read_rows = readout_ref.shape[0]
    block, hidden = features_ref.shape[1:]
    me = lax.axis_index("row") * sizes[1] + lax.axis_index("col")
    barrier = greet(sizes)

    def graph_copy(step, target, slot):
        where, _, _ = partners(step, sizes)
        return pltpu.make_async_remote_copy(
            src_ref=sent.at[target],
            dst_ref=arrived.at[slot],
            send_sem=send_sem.at[step],
            recv_sem=recv_sem.at[step],
            device_id=where,
            device_id_type=MESH,
        )

    def terms_copy(step, target, slot):
        where, _, _ = partners(step, sizes)
        return pltpu.make_async_remote_copy(
            src_ref=terms.at[target],
            dst_ref=terms_in.at[slot],
            send_sem=terms_send_sem.at[step],
            recv_sem=terms_recv_sem.at[step],
            device_id=where,
            device_id_type=MESH,
        )

    node_rows = lax.broadcasted_iota(jnp.int32, (block, edges_ref.shape[2]), 0)
    node_index = lax.broadcasted_iota(jnp.int32, (block, hidden), 0)

    def compute(target, store):
        blends = []
        for j in range(bucket):
            graph = picked_ref[target * bucket + j]
            features = features_ref[graph]
            edges = edges_ref[graph]
            sources = (node_rows == edges[0:1, :]).astype(jnp.float32).astype(jnp.bfloat16)
            targets = (node_rows == edges[1:2, :]).astype(jnp.float32).astype(jnp.bfloat16)
            adjacency = lax.dot_general(
                targets,
                sources,
                (((1,), (1,)), ((), ())),
                preferred_element_type=jnp.float32,
            ).astype(jnp.bfloat16)
            neighbour = jnp.dot(adjacency, features, preferred_element_type=jnp.float32)
            blends.append(
                (weight_ref[0] * features.astype(jnp.float32) + neighbour).astype(jnp.bfloat16)
            )
        blended = jnp.concatenate(blends, axis=0) if bucket > 1 else blends[0]
        hidden_one = jnp.maximum(
            jnp.dot(blended, w_first_ref[...], preferred_element_type=jnp.float32)
            + b_first_ref[...],
            0.0,
        ).astype(jnp.bfloat16)
        hidden_two = jnp.maximum(
            jnp.dot(hidden_one, w_second_ref[...], preferred_element_type=jnp.float32)
            + b_second_ref[...],
            0.0,
        ).astype(jnp.bfloat16)
        result = (
            jnp.dot(hidden_two, w_third_ref[...], preferred_element_type=jnp.float32)
            + b_third_ref[...]
        )
        for j in range(bucket):
            count = counts_ref[picked_ref[target * bucket + j]]
            rows = jnp.where(node_index < count, result[j * block : (j + 1) * block], 0.0)
            rows = rows.astype(jnp.bfloat16)
            store(j, rows)
            total = jnp.sum(rows.astype(jnp.float32), axis=0, keepdims=True)
            pooled[target * bucket + j] = total / jnp.full((1, hidden), count).astype(jnp.float32)

    pl.semaphore_wait(barrier, devices - 1)

    def compute_and_send(step, carry):
        _, target, _ = partners(step, sizes)

        def store(j, rows):
            sent[target, j] = rows

        compute(target, store)
        graph_copy(step, target, me).start()
        return carry

    lax.fori_loop(1, devices, compute_and_send, 0)

    def store_own(j, rows):
        arrived[me, j] = rows

    compute(me, store_own)

    slots = devices * bucket
    keys = lax.broadcasted_iota(jnp.int32, (devices * read_rows, slots), 0)
    members = (keys == ids_ref[...]).astype(jnp.float32)
    all_terms = jnp.dot(
        members,
        pooled[...].reshape(slots, hidden),
        precision=lax.Precision.HIGHEST,
        preferred_element_type=jnp.float32,
    )
    terms[...] = all_terms.reshape(devices, read_rows, hidden)

    def send_terms(step, carry):
        _, target, _ = partners(step, sizes)
        terms_copy(step, target, me).start()
        return carry

    lax.fori_loop(1, devices, send_terms, 0)
    terms_in[me] = terms[me]

    def finish(step, carry):
        _, target, source = partners(step, sizes)
        graph_copy(step, target, me).wait_send()
        graph_copy(step, target, source).wait_recv()
        terms_copy(step, target, me).wait_send()
        terms_copy(step, target, source).wait_recv()
        return carry

    lax.fori_loop(1, devices, finish, 0)
    readout_ref[...] = jnp.sum(terms_in[...], axis=0)

    def place(slot, carry):
        which = arrival_ref[slot]
        out_ref[slot] = arrived[which // bucket, which % bucket]
        return carry

    lax.fori_loop(0, out_ref.shape[0], place, 0)


def relay_kernel(
    sizes,
    bucket,
    units,
    most_units,
    table_ref,
    counts_ref,
    weight_ref,
    features_hbm_ref,
    edges_ref,
    ids_ref,
    w_first_ref,
    b_first_ref,
    w_second_ref,
    b_second_ref,
    w_third_ref,
    b_third_ref,
    out_ref,
    readout_ref,
    sent,
    arrived_a,
    arrived_b,
    arrived_c,
    arrived_d,
    packed,
    unpacked,
    pooled,
    terms,
    terms_in,
    plane_terms,
    final_terms,
    send_sem,
    recv_sem,
    relay_send_sem,
    relay_recv_sem,
    terms_send_sem,
    terms_recv_sem,
    final_send_sem,
    final_recv_sem,
    out_sem,
    features_ref,
    load_sem,
):
    rows_n, cols_n = sizes
    devices = rows_n * cols_n
    width = cols_n // PLANES
    in_plane = rows_n * width
    read_rows = readout_ref.shape[0]
    block, hidden = features_ref.shape[1:]
    parts = block // UNIT
    slots = devices * bucket
    pack_at = slots
    base_at = pack_at + PLANES * most_units
    size_at = base_at + out_ref.shape[0]
    plane_at = size_at + out_ref.shape[0]
    arrived = (arrived_a, arrived_b, arrived_c, arrived_d)
    row, col = lax.axis_index("row"), lax.axis_index("col")
    me = row * cols_n + col
    plane, lane = col // width, col % width
    own_place = row * width + lane
    barrier = greet(sizes)
    quarter = features_ref.shape[0] // 4
    loads = [
        pltpu.make_async_copy(
            features_hbm_ref.at[pl.ds(n * quarter, quarter)],
            features_ref.at[pl.ds(n * quarter, quarter)],
            load_sem.at[n],
        )
        for n in range(4)
    ]
    for load in loads:
        load.start()

    def other_plane(k):
        return (plane // 2 + k // 2) % 2 * 2 + (plane % 2 + k % 2) % 2

    def neighbour_at(step):
        to_row, to_lane = (row + step // width) % rows_n, (lane + step % width) % width
        from_row = (row + rows_n - step // width) % rows_n
        from_lane = (lane + width - step % width) % width
        return (to_row, plane * width + to_lane), to_row, to_lane, from_row * width + from_lane

    def graph_copy(number, k, step, place):
        where, _, _, _ = neighbour_at(step)
        return pltpu.make_async_remote_copy(
            src_ref=sent.at[number * in_plane + step],
            dst_ref=arrived[number].at[pl.ds(place * (bucket * parts), bucket * parts)],
            send_sem=send_sem.at[number * in_plane + step],
            recv_sem=recv_sem.at[number * in_plane + step],
            device_id=where,
            device_id_type=MESH,
        )

    def relay_copy(number, k, to_plane, from_plane):
        return pltpu.make_async_remote_copy(
            src_ref=packed.at[number],
            dst_ref=unpacked.at[pl.ds(from_plane * units, units)],
            send_sem=relay_send_sem.at[number],
            recv_sem=relay_recv_sem.at[number],
            device_id=(row, to_plane * width + lane),
            device_id_type=MESH,
        )

    def terms_copy(step, target, slot):
        where, _, _, _ = neighbour_at(step)
        return pltpu.make_async_remote_copy(
            src_ref=terms.at[target],
            dst_ref=terms_in.at[slot],
            send_sem=terms_send_sem.at[step],
            recv_sem=terms_recv_sem.at[step],
            device_id=where,
            device_id_type=MESH,
        )

    def final_copy(number, to_plane, from_plane):
        return pltpu.make_async_remote_copy(
            src_ref=plane_terms.at[to_plane],
            dst_ref=final_terms.at[from_plane],
            send_sem=final_send_sem.at[number],
            recv_sem=final_recv_sem.at[number],
            device_id=(row, to_plane * width + lane),
            device_id_type=MESH,
        )

    node_rows = lax.broadcasted_iota(jnp.int32, (block, edges_ref.shape[2]), 0)
    node_index = lax.broadcasted_iota(jnp.int32, (block, hidden), 0)

    def compute(target, store):
        blends = []
        for j in range(bucket):
            graph = table_ref[target * bucket + j]
            features = features_ref[graph]
            edges = edges_ref[graph]
            sources = (node_rows == edges[0:1, :]).astype(jnp.float32).astype(jnp.bfloat16)
            targets = (node_rows == edges[1:2, :]).astype(jnp.float32).astype(jnp.bfloat16)
            adjacency = lax.dot_general(
                targets,
                sources,
                (((1,), (1,)), ((), ())),
                preferred_element_type=jnp.float32,
            ).astype(jnp.bfloat16)
            neighbour = jnp.dot(adjacency, features, preferred_element_type=jnp.float32)
            blends.append(
                (weight_ref[0] * features.astype(jnp.float32) + neighbour).astype(jnp.bfloat16)
            )
        blended = jnp.concatenate(blends, axis=0) if bucket > 1 else blends[0]
        hidden_one = jnp.maximum(
            jnp.dot(blended, w_first_ref[...], preferred_element_type=jnp.float32)
            + b_first_ref[...],
            0.0,
        ).astype(jnp.bfloat16)
        hidden_two = jnp.maximum(
            jnp.dot(hidden_one, w_second_ref[...], preferred_element_type=jnp.float32)
            + b_second_ref[...],
            0.0,
        ).astype(jnp.bfloat16)
        result = (
            jnp.dot(hidden_two, w_third_ref[...], preferred_element_type=jnp.float32)
            + b_third_ref[...]
        )
        for j in range(bucket):
            count = counts_ref[table_ref[target * bucket + j]]
            rows = jnp.where(node_index < count, result[j * block : (j + 1) * block], 0.0)
            rows = rows.astype(jnp.bfloat16)
            store(j, rows.reshape(parts, UNIT, hidden))
            total = jnp.sum(rows.astype(jnp.float32), axis=0, keepdims=True)
            pooled[target * bucket + j] = total / jnp.full((1, hidden), count).astype(jnp.float32)

    def first_stage(number, k, lower, upper):
        def compute_and_send(step, carry):
            _, to_row, to_lane, _ = neighbour_at(step)

            def store(j, rows):
                sent[number * in_plane + step, pl.ds(j * parts, parts)] = rows

            compute(to_row * cols_n + other_plane(k) * width + to_lane, store)
            graph_copy(number, k, step, own_place).start()
            return carry

        lax.fori_loop(lower, upper, compute_and_send, 0)
        if upper < in_plane:
            return

        def store_own(j, rows):
            arrived[number][pl.ds((own_place * bucket + j) * parts, parts)] = rows

        compute(row * cols_n + other_plane(k) * width + lane, store_own)

    def second_stage(number, k):
        def finish(step, carry):
            _, _, _, source = neighbour_at(step)
            graph_copy(number, k, step, own_place).wait_send()
            graph_copy(number, k, step, source).wait_recv()
            return carry

        lax.fori_loop(1, in_plane, finish, 0)
        to_plane = other_plane(k)

        def pack(step, carry):
            for n in range(8):
                unit = step * 8 + n
                value = arrived[number][table_ref[pack_at + to_plane * most_units + unit]]
                if k == 0:
                    unpacked[plane * units + unit] = value
                else:
                    packed[number, unit] = value
            return carry

        lax.fori_loop(0, units // 8, pack, 0)
        if k != 0:
            relay_copy(number, k, to_plane, plane).start()

    pl.semaphore_wait(barrier, devices - 1)
    for load in loads:
        load.wait()
    for number, k in enumerate(CLASSES):
        if number == 1:
            first_stage(number, k, 1, in_plane // 2)
            second_stage(0, CLASSES[0])
            first_stage(number, k, in_plane // 2, in_plane)
        else:
            first_stage(number, k, 1, in_plane)
        if number > 1:
            second_stage(number - 1, CLASSES[number - 1])

    keys = lax.broadcasted_iota(jnp.int32, (devices * read_rows, slots), 0)
    members = (keys == ids_ref[...]).astype(jnp.float32)
    all_terms = jnp.dot(
        members,
        pooled[...].reshape(slots, hidden),
        precision=lax.Precision.HIGHEST,
        preferred_element_type=jnp.float32,
    )
    for place in range(in_plane):
        for to_plane in range(PLANES):
            device = place // width * cols_n + to_plane * width + place % width
            terms[place, to_plane] = all_terms[device * read_rows : (device + 1) * read_rows]

    def send_terms(step, carry):
        _, to_row, to_lane, _ = neighbour_at(step)
        terms_copy(step, to_row * width + to_lane, own_place).start()
        return carry

    lax.fori_loop(1, in_plane, send_terms, 0)
    terms_in[own_place] = terms[own_place]
    second_stage(PLANES - 1, CLASSES[PLANES - 1])

    def finish_terms(step, carry):
        _, to_row, to_lane, source = neighbour_at(step)
        terms_copy(step, to_row * width + to_lane, own_place).wait_send()
        terms_copy(step, to_row * width + to_lane, source).wait_recv()
        return carry

    lax.fori_loop(1, in_plane, finish_terms, 0)
    plane_terms[...] = jnp.sum(terms_in[...], axis=0)
    final_terms[plane] = plane_terms[plane]
    for number, k in enumerate(CLASSES):
        if k != 0:
            final_copy(number, other_plane(k), plane).start()
    for number, k in enumerate(CLASSES):
        if k != 0:
            relay_copy(number, k, other_plane(k), plane).wait_send()
            relay_copy(number, k, other_plane(k), other_plane(k)).wait_recv()

    def out_copy(slot):
        return pltpu.make_async_copy(
            sent.at[slot // bucket, pl.ds(slot % bucket * parts, parts)],
            out_ref.at[slot],
            out_sem.at[slot],
        )

    def place_graph(slot, carry):
        base = table_ref[base_at + slot] + table_ref[plane_at + slot] * units
        size = table_ref[size_at + slot]
        for part in range(parts):
            value = unpacked[jnp.minimum(base + part, PLANES * units - 1)]
            value = jnp.where(jnp.full((UNIT, hidden), size) > part, value, jnp.zeros_like(value))
            sent[slot // bucket, slot % bucket * parts + part] = value
        out_copy(slot).start()
        return carry

    lax.fori_loop(0, out_ref.shape[0], place_graph, 0)
    for number, k in enumerate(CLASSES):
        if k != 0:
            final_copy(number, other_plane(k), plane).wait_send()
            final_copy(number, other_plane(k), other_plane(k)).wait_recv()
    readout_ref[...] = jnp.sum(final_terms[...], axis=0)

    def finish_out(slot, carry):
        out_copy(slot).wait()
        return carry

    lax.fori_loop(0, out_ref.shape[0], finish_out, 0)


def body(
    sizes,
    node_features,
    node_counts,
    edge_list,
    readout_ids,
    live_graphs,
    self_weight,
    w_first,
    b_first,
    w_second,
    b_second,
    w_third,
    b_third,
):
    rows_n, cols_n = sizes
    devices = rows_n * cols_n
    width = cols_n // PLANES
    in_plane = rows_n * width
    capacity, block, hidden = node_features.shape
    parts = block // UNIT
    graphs_out = capacity // 2
    read_rows = 8
    bucket = (capacity + devices - 1) // devices
    slots_n = devices * bucket
    mean_units = graphs_out * parts // PLANES
    caps = [mean_units * eighths // 64 * 8 for eighths in (8, 9, 10)]
    units = caps[-1]
    own_count = live_graphs[0]
    row, col = lax.axis_index("row"), lax.axis_index("col")
    plane, lane = col // width, col % width
    me = row * cols_n + col
    every = gather_counts(node_counts, live_graphs, sizes)
    every_count = every[:, capacity]
    earlier = jnp.arange(devices)[:, None] >= jnp.arange(devices)[None, :]
    inclusive = jnp.sum(jnp.where(earlier, every_count[None, :], 0), axis=1)
    offsets = inclusive - every_count
    offset = jnp.sum(jnp.where(jnp.arange(devices) == me, offsets, 0))
    slots = lax.broadcasted_iota(jnp.int32, (slots_n,), 0)
    within = (slots // bucket - offset) % devices + slots % bucket * devices
    picked = jnp.minimum(within, capacity - 1)
    choose = picked[:, None] == jnp.arange(capacity)[None, :]
    picked_ids = jnp.sum(jnp.where(choose, readout_ids[None, :], 0), axis=1)
    graph_ids = jnp.where(within < own_count, picked_ids, -1).reshape(1, -1)
    number = lax.broadcasted_iota(jnp.int32, (graphs_out,), 0) * devices + me
    passed = (inclusive[None, :] <= number[:, None]).astype(jnp.int32)
    source = jnp.sum(passed, axis=1)
    start = jnp.sum(passed * every_count[None, :], axis=1)
    turn = (number - start) // devices

    index = jnp.arange(capacity)[None, :]
    sizes_all = jnp.where(
        index < every_count[:, None], (every[:, :capacity] + (UNIT - 1)) // UNIT, 0
    )
    dests = (offsets[:, None] + index) % devices
    by_dest = jnp.sum(
        jnp.where(dests[:, :, None] == jnp.arange(devices), sizes_all[:, :, None], 0), axis=1
    )
    plane_load = jnp.sum(by_dest.reshape(rows_n, PLANES, width, devices), axis=(0, 2))
    most = jnp.max(plane_load)
    tier = sum((most > cap).astype(jnp.int32) for cap in caps)

    turns = jnp.arange(bucket)[:, None] == index // devices

    def by_plane(values):
        values = values.reshape(rows_n, PLANES, width, capacity)
        return jnp.swapaxes(values, 0, 1).reshape(PLANES, in_plane, capacity)

    plane_sizes, plane_dests = by_plane(sizes_all), by_plane(dests)
    own_sizes = lax.dynamic_index_in_dim(plane_sizes, plane, 0, keepdims=False)
    own_dests = lax.dynamic_index_in_dim(plane_dests, plane, 0, keepdims=False)

    def slot_sizes(values, wanted):
        chosen = wanted[:, :, None, :] & turns
        return jnp.sum(jnp.where(chosen, values[:, :, None, :], 0), axis=3).reshape(PLANES, -1)

    relay_dests = row * cols_n + jnp.arange(PLANES) * width + lane
    relay_sizes = slot_sizes(own_sizes[None], own_dests[None] == relay_dests[:, None, None])
    final_sizes = slot_sizes(plane_sizes, plane_dests == me)
    places = in_plane * bucket
    before = jnp.arange(places)[:, None] >= jnp.arange(places)[None, :]

    def ends(values):
        return jnp.sum(jnp.where(before, values[:, None, :], 0), axis=2)

    done = ends(relay_sizes)[:, None, :] <= jnp.arange(units)[None, :, None]
    slot_of = jnp.minimum(jnp.sum(done.astype(jnp.int32), axis=2), places - 1)
    part_of = jnp.arange(units) - jnp.sum(jnp.where(done, relay_sizes[:, None, :], 0), axis=2)
    pack = slot_of * parts + jnp.clip(part_of, 0, parts - 1)
    starts = ends(final_sizes) - final_sizes
    source_row, source_col = source // cols_n, source % cols_n
    place = (source_row * width + source_col % width) * bucket + turn
    place = source_col // width * places + place
    match = place[:, None] == jnp.arange(PLANES * places)[None, :]
    base = jnp.sum(jnp.where(match, starts.reshape(1, -1), 0), axis=1)
    size = jnp.sum(jnp.where(match, final_sizes.reshape(1, -1), 0), axis=1)
    table = jnp.concatenate([picked, pack.reshape(-1), base, size, source_col // width]).astype(jnp.int32)
    arrival = (source * bucket + turn).astype(jnp.int32)

    out_shape = (
        jax.ShapeDtypeStruct((graphs_out, block, hidden), jnp.bfloat16),
        jax.ShapeDtypeStruct((read_rows, hidden), jnp.float32),
    )
    pooled_scratch = pltpu.VMEM((slots_n, 1, hidden), jnp.float32)

    def semaphores(count):
        return [pltpu.SemaphoreType.DMA((count,)), pltpu.SemaphoreType.DMA((count,))]

    def relayed(tier, units, *operands):
        table, _, node_counts = operands[:3]
        graphs = pltpu.VMEM((in_plane * bucket * parts, UNIT, hidden), jnp.bfloat16)
        whole_terms = pltpu.VMEM((in_plane, PLANES, read_rows, hidden), jnp.float32)
        some_terms = pltpu.VMEM((PLANES, read_rows, hidden), jnp.float32)
        node_out, readout = pl.pallas_call(
            functools.partial(relay_kernel, sizes, bucket, units, caps[-1]),
            out_shape=(
                jax.ShapeDtypeStruct((graphs_out, parts, UNIT, hidden), jnp.bfloat16),
                out_shape[1],
            ),
            in_specs=[SMEM] * 3 + [HBM] + [VMEM] * 8,
            out_specs=(HBM, VMEM),
            scratch_shapes=[
                pltpu.VMEM((devices, bucket * parts, UNIT, hidden), jnp.bfloat16),
                graphs,
                graphs,
                graphs,
                graphs,
                pltpu.VMEM((PLANES - 1, units, UNIT, hidden), jnp.bfloat16),
                pltpu.VMEM((PLANES * units, UNIT, hidden), jnp.bfloat16),
            ]
            + [pooled_scratch, whole_terms, whole_terms, some_terms, some_terms]
            + semaphores(devices)
            + semaphores(PLANES)
            + semaphores(in_plane)
            + semaphores(PLANES)
            + [
                pltpu.SemaphoreType.DMA((graphs_out,)),
                pltpu.VMEM((capacity, block, hidden), jnp.bfloat16),
                pltpu.SemaphoreType.DMA((4,)),
            ],
            compiler_params=pltpu.CompilerParams(
                collective_id=2 + tier, has_side_effects=True, vmem_limit_bytes=61 * 1024 * 1024
            ),
            name="gin_relay",
        )(table, node_counts, *operands[3:])
        return node_out.reshape(graphs_out, block, hidden), readout

    def direct(*operands):
        table, arrival, node_counts = operands[:3]
        all_terms = pltpu.VMEM((devices, read_rows, hidden), jnp.float32)
        graphs = pltpu.VMEM((devices, bucket, block, hidden), jnp.bfloat16)
        return pl.pallas_call(
            functools.partial(layer_kernel, sizes, bucket),
            out_shape=out_shape,
            in_specs=[SMEM] * 4 + [VMEM] * 9,
            out_specs=(VMEM, VMEM),
            scratch_shapes=[graphs, graphs]
            + [pooled_scratch, all_terms, all_terms]
            + semaphores(devices)
            + semaphores(devices),
            compiler_params=pltpu.CompilerParams(
                collective_id=1, has_side_effects=True, vmem_limit_bytes=60 * 1024 * 1024
            ),
            name="gin_direct",
        )(table[:slots_n], node_counts, arrival, *operands[3:])

    branches = [functools.partial(relayed, number, cap) for number, cap in enumerate(caps)]
    return lax.switch(
        tier,
        branches + [direct],
        table,
        arrival,
        node_counts,
        self_weight,
        node_features,
        edge_list,
        graph_ids,
        w_first,
        b_first.reshape(1, -1),
        w_second,
        b_second.reshape(1, -1),
        w_third,
        b_third.reshape(1, -1),
    )


def solution(mesh):
    sizes = (mesh.shape["row"], mesh.shape["col"])
    both = ("row", "col")
    in_specs = (
        P(both, None, None),
        P(both),
        P(both, None, None),
        P(both),
        P(both),
        P(),
        P(),
        P(),
        P(),
        P(),
        P(),
        P(),
    )
    out_specs = (P(both, None, None), P(both, None))
    return jax.shard_map(
        functools.partial(body, sizes),
        mesh=mesh,
        in_specs=in_specs,
        out_specs=out_specs,
        check_vma=False,
    )
```
